32 devices in a mesh: dp: 4 (over y, x), tile: 8 (over z, core).
Axes of the slice: x: 2, y: 2, z: 4, core: 2. Of those that a mesh axis runs over, the one named last changes fastest.
Arguments:
- features: bfloat16 [4, 8, 512, 1280], P('dp', 'tile'), may hold values from -6 to 6
- visible: int32 [4, 8, 512], P('dp', 'tile'), may hold values from 0 to 1, as said below
- positions: int32 [4, 8, 512], P('dp', 'tile'), may hold values from 0 to 511, each once within a row
- cotangent: bfloat16 [4, 8, 512, 512], P('dp', 'tile'), may hold values from -6 to 6
- mlp_gain: float32 [1280], replicated, may hold values from 0.1 to 1.9
- mlp_bias: float32 [1280], replicated, may hold values from -3 to 3
- fc1_weight: bfloat16 [1280, 2560], replicated, may hold values from -0.15625 to 0.15625
- fc1_bias: float32 [2560], replicated, may hold values from -3 to 3
- fc2_weight: bfloat16 [2560, 1280], replicated, may hold values from -0.125 to 0.125
- fc2_bias: float32 [1280], replicated, may hold values from -3 to 3
- encoder_gain: float32 [1280], replicated, may hold values from 0.1 to 1.9
- encoder_bias: float32 [1280], replicated, may hold values from -3 to 3
- embed_weight: bfloat16 [1280, 512], replicated, may hold values from -0.15625 to 0.15625
- embed_bias: float32 [512], replicated, may hold values from -3 to 3
- mask_token: float32 [512], replicated, may hold values from -4 to 4
- position_table: bfloat16 [512, 512], replicated, may hold values from -4 to 4
- decoder_gain: float32 [512], replicated, may hold values from 0.1 to 1.9
- decoder_bias: float32 [512], replicated, may hold values from -3 to 3
Outputs:
- feature_grad: bfloat16 [4, 8, 512, 1280], P('dp', 'tile')
- decoded: bfloat16 [4, 8, 512, 512], P('dp', 'tile')
- fc1_grad: float32 [1280, 2560], P('tile')
- fc2_grad: float32 [2560, 1280], P('tile')
The draws below stay inside these ranges and needn't reach their ends.
Inputs may be any that keep to these rules, and one draw needn't show every extreme that they name: In each scene (all 8 chips of one index of the first dimension) exactly 1024 patches are visible; each chip has at most 256 visible patches, and in every scene one chip has exactly 256. Each chip's position ids are a permutation of its 512 positions.
All inputs are finite; a program needn't handle non-finite values.
Results may differ from the reference program's by a relative error of at most 0.007.
Values may be sent and summed in bfloat16 or wider, within the bound.
A program may use at most 128 MiB of HBM per device.

```python
import jax
import jax.numpy as jnp
from jax import lax

D = 1280
DD = 512
HID = 2560
PATCHES = 512
SCENES = 4
TILES = 8
KEEP = 1024
MOST = 256
N_DP = 4
N_TILE = 8


def draw_visible(key, part):

    def one_scene(scene_key):
        key_busy, key_weight, key_perm = jax.random.split(scene_key, 3)
        tile_ids = jnp.arange(TILES, dtype=jnp.int32)
        busiest = jax.random.randint(key_busy, (), 0, TILES, dtype=jnp.int32)
        weights = jax.random.randint(key_weight, (TILES,), 2, 5, dtype=jnp.int32)
        weights = jnp.where(tile_ids == busiest, 0, weights)
        remain = KEEP - MOST
        portion = remain * weights // jnp.sum(weights)
        leftover = remain - jnp.sum(portion)
        others_rank = jnp.cumsum((weights > 0).astype(jnp.int32)) - 1
        portion = portion + ((weights > 0) & (others_rank < leftover)).astype(jnp.int32)
        chip_counts = jnp.where(tile_ids == busiest, MOST, portion)
        perm_keys = jax.random.split(key_perm, TILES)

        def one_chip(chip_key):
            return jax.random.permutation(chip_key, PATCHES).astype(jnp.int32)
        priority = jax.vmap(one_chip)(perm_keys)
        return (priority < chip_counts[:, None]).astype(jnp.int32)
    scene_keys = jax.random.split(key, SCENES)
    return jax.vmap(one_scene)(scene_keys)


def shard_levels(rng, shape, shards, low, high):
    factor_of, own = 1.0, jax.random.fold_in(rng, 6)
    for axis_at, parts in shards:
        steps = jnp.exp(jax.random.uniform(jax.random.fold_in(own, axis_at), (parts,), jnp.float32, low / len(shards), high / len(shards)))
        factor_of = factor_of * jnp.repeat(steps, shape[axis_at] // parts).reshape([-1 if axis == axis_at else 1 for axis in range(len(shape))])
    return factor_of


def noise(rng, extent, deviation, limit, cuts=(), held_as=jnp.bfloat16):
    drawn = jax.random.normal(rng, extent, jnp.float32) * deviation
    if len(cuts) > 0:
        drawn = shard_levels(rng, extent, cuts, -0.22, 0.18) * drawn
    return jnp.clip(drawn, min=-limit, max=limit).astype(held_as)


def setup_inputs(seed: int = 0) -> dict:
    seeds = jax.random.split(jax.random.key(seed), 19)
    features = noise(seeds[0], (SCENES, TILES, PATCHES, D), 1.0, 6.0, ((0, 4), (1, 8)))
    visible = draw_visible(jax.random.fold_in(seeds[18], 71), 0)
    positions = jax.vmap(lambda own: jax.random.permutation(own, PATCHES))(jax.random.split(seeds[2], SCENES * TILES)).reshape((SCENES, TILES, PATCHES)).astype(jnp.int32)
    cotangent = noise(seeds[3], (SCENES, TILES, PATCHES, DD), 1.0, 6.0, ((0, 4), (1, 8)))
    mlp_gain = jnp.clip(1.0 + 0.18 * jax.random.normal(seeds[4], (D,), jnp.float32), 0.1, 1.9)
    mlp_bias = noise(seeds[5], (D,), 0.5, 3.0, (), jnp.float32)
    fc1_weight = noise(seeds[6], (D, HID), D ** -0.5, 0.15625)
    fc1_bias = noise(seeds[7], (HID,), 0.5, 3.0, (), jnp.float32)
    fc2_weight = noise(seeds[8], (HID, D), HID ** -0.5, 0.125)
    fc2_bias = noise(seeds[9], (D,), 0.5, 3.0, (), jnp.float32)
    encoder_gain = jnp.clip(1.0 + 0.18 * jax.random.normal(seeds[10], (D,), jnp.float32), 0.1, 1.9)
    encoder_bias = noise(seeds[11], (D,), 0.5, 3.0, (), jnp.float32)
    embed_weight = noise(seeds[12], (D, DD), D ** -0.5, 0.15625)
    embed_bias = noise(seeds[13], (DD,), 0.5, 3.0, (), jnp.float32)
    mask_token = noise(seeds[14], (DD,), 1.0, 4.0, (), jnp.float32)
    position_table = noise(seeds[15], (PATCHES, DD), 0.7, 4.0)
    decoder_gain = jnp.clip(1.0 + 0.18 * jax.random.normal(seeds[16], (DD,), jnp.float32), 0.1, 1.9)
    decoder_bias = noise(seeds[17], (DD,), 0.5, 3.0, (), jnp.float32)
    return {"features": features, "visible": visible, "positions": positions, "cotangent": cotangent, "mlp_gain": mlp_gain, "mlp_bias": mlp_bias, "fc1_weight": fc1_weight, "fc1_bias": fc1_bias, "fc2_weight": fc2_weight, "fc2_bias": fc2_bias, "encoder_gain": encoder_gain, "encoder_bias": encoder_bias, "embed_weight": embed_weight, "embed_bias": embed_bias, "mask_token": mask_token, "position_table": position_table, "decoder_gain": decoder_gain, "decoder_bias": decoder_bias}


epsilon = 1e-06

def layer_norm(values, norm_gain, norm_bias):
    row_mean = lax.optimization_barrier(jnp.mean(values, axis=-1, keepdims=True))
    centred = values - row_mean
    variance = lax.optimization_barrier(jnp.mean(centred * centred, axis=-1, keepdims=True))
    inv_std = lax.rsqrt(variance + epsilon)
    scaled = centred * inv_std
    return (scaled * norm_gain + norm_bias, scaled, inv_std)

def norm_back(upstream, scaled, inv_std):
    mean_up = lax.optimization_barrier(jnp.mean(upstream, axis=-1, keepdims=True))
    mean_cross = lax.optimization_barrier(jnp.mean(upstream * scaled, axis=-1, keepdims=True))
    return inv_std * (upstream - mean_up - scaled * mean_cross)

def gelu_parts(pre_act):
    normal_cdf = 0.5 * (1.0 + lax.erf(pre_act * 0.7071067811865476))
    density = jnp.exp(-0.5 * pre_act * pre_act) * 0.3989422804014327
    return (pre_act * normal_cdf, normal_cdf + pre_act * density)

def reference(features, visible, positions, cotangent, mlp_gain, mlp_bias, fc1_weight, fc1_bias, fc2_weight, fc2_bias, encoder_gain, encoder_bias, embed_weight, embed_bias, mask_token, position_table, decoder_gain, decoder_bias):
    row_count = TILES * PATCHES

    def scene_step(carry, inputs):
        fc1_sum, fc2_sum = carry
        scene_feats, scene_vis, scene_pos, scene_cot = inputs
        row_data = scene_feats.reshape(-1, D)
        flags = scene_vis.reshape(-1).astype(jnp.int32)
        keep_rows = (flags > 0)[:, None]
        rank = jnp.cumsum(flags).astype(jnp.int32) - flags
        target = jnp.where(flags > 0, rank, row_count).astype(jnp.int32)
        order = jnp.zeros((row_count,), jnp.int32).at[target].set(jnp.arange(row_count, dtype=jnp.int32), mode='drop')
        compact = order[:KEEP]
        rows_in = jnp.take(row_data, compact, axis=0).astype(jnp.float32)
        mlp_in, mlp_scaled, mlp_inv = layer_norm(rows_in, mlp_gain, mlp_bias)
        mlp_in = mlp_in.astype(jnp.bfloat16)
        pre_act = jnp.dot(mlp_in, fc1_weight, preferred_element_type=jnp.float32) + fc1_bias
        activation, slope = gelu_parts(pre_act)
        hidden = activation.astype(jnp.bfloat16)
        encoded = rows_in + jnp.dot(hidden, fc2_weight, preferred_element_type=jnp.float32) + fc2_bias
        normed, enc_scaled, enc_inv = layer_norm(encoded, encoder_gain, encoder_bias)
        normed = normed.astype(jnp.bfloat16)
        projected = (jnp.dot(normed, embed_weight, preferred_element_type=jnp.float32) + embed_bias).astype(jnp.bfloat16)
        projected_full = jnp.zeros((row_count, DD), jnp.bfloat16).at[compact].set(projected)
        placed = jnp.take(position_table, scene_pos.reshape(-1), axis=0).astype(jnp.float32)
        dec_input = jnp.where(keep_rows, projected_full.astype(jnp.float32), mask_token) + placed
        decoded, dec_scaled, dec_inv = layer_norm(dec_input, decoder_gain, decoder_bias)
        upstream = scene_cot.reshape(-1, DD).astype(jnp.float32)
        grad_input = norm_back(upstream * decoder_gain, dec_scaled, dec_inv)
        grad_projected = jnp.where(keep_rows, grad_input, 0.0).astype(jnp.bfloat16)
        grad_compact = jnp.take(grad_projected, compact, axis=0)
        grad_normed = jnp.dot(grad_compact, embed_weight.T, preferred_element_type=jnp.float32)
        grad_encoded = norm_back(grad_normed * encoder_gain, enc_scaled, enc_inv).astype(jnp.bfloat16)
        grad_hidden = jnp.dot(grad_encoded, fc2_weight.T, preferred_element_type=jnp.float32)
        grad_pre = (grad_hidden * slope).astype(jnp.bfloat16)
        grad_mlp_in = jnp.dot(grad_pre, fc1_weight.T, preferred_element_type=jnp.float32)
        grad_feats = (grad_encoded.astype(jnp.float32) + norm_back(grad_mlp_in * mlp_gain, mlp_scaled, mlp_inv)).astype(jnp.bfloat16)
        fc1_term = jnp.dot(mlp_in.T, grad_pre, preferred_element_type=jnp.float32)
        fc2_term = jnp.dot(hidden.T, grad_encoded, preferred_element_type=jnp.float32)
        grad_rows = jnp.zeros((row_count, D), jnp.bfloat16).at[compact].set(grad_feats)
        outputs = (grad_rows.reshape(TILES, PATCHES, D), decoded.astype(jnp.bfloat16).reshape(TILES, PATCHES, DD))
        return ((fc1_sum + fc1_term, fc2_sum + fc2_term), outputs)
    start_carry = (jnp.zeros((D, HID), jnp.float32), jnp.zeros((HID, D), jnp.float32))
    final_carry, stacked = lax.scan(scene_step, start_carry, (features, visible, positions, cotangent))
    fc1_sum, fc2_sum = final_carry
    feature_grad, decoded = stacked
    device_total = N_DP * N_TILE
    return (feature_grad, decoded, fc1_sum / device_total, fc2_sum / device_total)
```

```python
import jax
import jax.numpy as jnp
from jax import lax
from jax.sharding import PartitionSpec as P

epsilon = 1e-06


def layer_norm(values, norm_gain, norm_bias):
    row_mean = jnp.mean(values, axis=-1, keepdims=True)
    centred = values - row_mean
    variance = jnp.mean(centred * centred, axis=-1, keepdims=True)
    inv_std = lax.rsqrt(variance + epsilon)
    scaled = centred * inv_std
    return (scaled * norm_gain + norm_bias, scaled, inv_std)


def norm_back(upstream, scaled, inv_std):
    mean_up = jnp.mean(upstream, axis=-1, keepdims=True)
    mean_cross = jnp.mean(upstream * scaled, axis=-1, keepdims=True)
    return inv_std * (upstream - mean_up - scaled * mean_cross)


def gelu_parts(pre_act):
    normal_cdf = 0.5 * (1.0 + lax.erf(pre_act * 0.7071067811865476))
    density = jnp.exp(-0.5 * pre_act * pre_act) * 0.3989422804014327
    return (pre_act * normal_cdf, normal_cdf + pre_act * density)


def encode(enc_input, enc_params):
    (
        mlp_gain,
        mlp_bias,
        fc1_weight,
        fc1_bias,
        fc2_weight,
        fc2_bias,
        encoder_gain,
        encoder_bias,
        embed_weight,
        embed_bias,
    ) = enc_params
    rows_in = enc_input.astype(jnp.float32)
    mlp_in, mlp_scaled, mlp_inv = layer_norm(rows_in, mlp_gain, mlp_bias)
    mlp_in = mlp_in.astype(jnp.bfloat16)
    pre_act = jnp.dot(mlp_in, fc1_weight, preferred_element_type=jnp.float32) + fc1_bias
    activation, slope = gelu_parts(pre_act)
    hidden = activation.astype(jnp.bfloat16)
    encoded = rows_in + jnp.dot(hidden, fc2_weight, preferred_element_type=jnp.float32) + fc2_bias
    normed, enc_scaled, enc_inv = layer_norm(encoded, encoder_gain, encoder_bias)
    normed = normed.astype(jnp.bfloat16)
    projected = (
        jnp.dot(normed, embed_weight, preferred_element_type=jnp.float32) + embed_bias
    ).astype(jnp.bfloat16)
    saved = (mlp_in, mlp_scaled, mlp_inv, slope, hidden, enc_scaled, enc_inv)
    return (saved, projected)


def encode_back(saved, grad_compact, enc_params):
    (
        mlp_gain,
        mlp_bias,
        fc1_weight,
        fc1_bias,
        fc2_weight,
        fc2_bias,
        encoder_gain,
        encoder_bias,
        embed_weight,
        embed_bias,
    ) = enc_params
    mlp_in, mlp_scaled, mlp_inv, slope, hidden, enc_scaled, enc_inv = saved
    grad_normed = jnp.dot(grad_compact, embed_weight.T, preferred_element_type=jnp.float32)
    grad_encoded = norm_back(grad_normed * encoder_gain, enc_scaled, enc_inv).astype(jnp.bfloat16)
    grad_hidden = jnp.dot(grad_encoded, fc2_weight.T, preferred_element_type=jnp.float32)
    grad_pre = (grad_hidden * slope).astype(jnp.bfloat16)
    grad_mlp_in = jnp.dot(grad_pre, fc1_weight.T, preferred_element_type=jnp.float32)
    grad_feats = (
        grad_encoded.astype(jnp.float32) + norm_back(grad_mlp_in * mlp_gain, mlp_scaled, mlp_inv)
    ).astype(jnp.bfloat16)
    fc1_term = jnp.dot(mlp_in.T, grad_pre, preferred_element_type=jnp.float32)
    fc2_term = jnp.dot(hidden.T, grad_encoded, preferred_element_type=jnp.float32)
    return (fc1_term, fc2_term, grad_feats)


def decoder_pass(
    projected_rows,
    keep_rows,
    position_ids,
    upstream,
    position_table,
    mask_token,
    decoder_gain,
    decoder_bias,
):
    table_ids = jnp.arange(position_table.shape[0], dtype=jnp.int32)[None, :]
    pick = (position_ids[:, None] == table_ids).astype(jnp.bfloat16)
    placed = jnp.dot(pick, position_table, preferred_element_type=jnp.float32)
    dec_input = jnp.where(keep_rows, projected_rows, mask_token) + placed
    decoded, dec_scaled, dec_inv = layer_norm(dec_input, decoder_gain, decoder_bias)
    grad_input = norm_back(upstream.astype(jnp.float32) * decoder_gain, dec_scaled, dec_inv)
    grad_projected = jnp.where(keep_rows, grad_input, 0.0).astype(jnp.bfloat16)
    return (decoded.astype(jnp.bfloat16), grad_projected)


def shards(
    features,
    visible,
    positions,
    cotangent,
    mlp_gain,
    mlp_bias,
    fc1_weight,
    fc1_bias,
    fc2_weight,
    fc2_bias,
    encoder_gain,
    encoder_bias,
    embed_weight,
    embed_bias,
    mask_token,
    position_table,
    decoder_gain,
    decoder_bias,
):
    patch_count = features.shape[2]
    model_width = features.shape[3]
    dec_width = embed_weight.shape[1]
    most_rows = patch_count // 2
    flags = visible.reshape(patch_count)
    row_data = features.reshape(patch_count, model_width)
    keep_rows = (flags > 0)[:, None]
    upstream = cotangent.reshape(patch_count, dec_width)
    ids = jnp.arange(patch_count, dtype=jnp.int32)
    row_rank = jnp.sum(jnp.where(ids[None, :] < ids[:, None], flags[None, :], 0), axis=1)
    slots = jnp.arange(most_rows, dtype=jnp.int32)
    target = jnp.where(flags > 0, row_rank, -1)
    gather = (slots[:, None] == target[None, :]).astype(jnp.bfloat16)
    scatter = (target[:, None] == slots[None, :]).astype(jnp.bfloat16)
    enc_params = (
        mlp_gain,
        mlp_bias,
        fc1_weight,
        fc1_bias,
        fc2_weight,
        fc2_bias,
        encoder_gain,
        encoder_bias,
        embed_weight,
        embed_bias,
    )
    decoder_args = (position_table, mask_token, decoder_gain, decoder_bias)
    enc_input = jnp.dot(gather, row_data, preferred_element_type=jnp.bfloat16)
    saved, projected = encode(enc_input, enc_params)
    projected_rows = jnp.dot(scatter, projected, preferred_element_type=jnp.float32)
    decoded, grad_projected = decoder_pass(
        projected_rows, keep_rows, positions.reshape(-1), upstream, *decoder_args
    )
    grad_compact = jnp.dot(gather, grad_projected, preferred_element_type=jnp.bfloat16)
    fc1_term, fc2_term, grad_feats = encode_back(saved, grad_compact, enc_params)
    grad_rows = jnp.dot(scatter, grad_feats, preferred_element_type=jnp.bfloat16)
    device_total = lax.axis_size("dp") * lax.axis_size("tile")
    totals = []
    for term in (fc1_term, fc2_term):
        share = lax.psum_scatter(
            term.astype(jnp.bfloat16), "tile", scatter_dimension=0, tiled=True
        )
        totals.append(lax.psum(share, "dp").astype(jnp.float32) / device_total)
    fc1_grad, fc2_grad = totals
    feature_grad = grad_rows.reshape(features.shape)
    decoded_out = decoded.reshape(cotangent.shape)
    return (feature_grad, decoded_out, fc1_grad, fc2_grad)


def solution(mesh):
    return jax.shard_map(
        shards,
        mesh=mesh,
        in_specs=(
            P("dp", "tile", None, None),
            P("dp", "tile", None),
            P("dp", "tile", None),
            P("dp", "tile", None, None),
            P(),
            P(),
            P(),
            P(),
            P(),
            P(),
            P(),
            P(),
            P(),
            P(),
            P(),
            P(),
            P(),
            P(),
        ),
        out_specs=(
            P("dp", "tile", None, None),
            P("dp", "tile", None, None),
            P("tile", None),
            P("tile", None),
        ),
        check_vma=False,
    )
```

```python
import functools

import jax
import jax.numpy as jnp
from jax import lax
from jax.experimental import pallas as pl
from jax.experimental.pallas import tpu as pltpu
from jax.sharding import PartitionSpec as P

MESH = pl.DeviceIdType.MESH

epsilon = 1e-06


def layer_norm(values, norm_gain, norm_bias):
    row_mean = jnp.mean(values, axis=-1, keepdims=True)
    centred = values - row_mean
    variance = jnp.mean(centred * centred, axis=-1, keepdims=True)
    inv_std = lax.rsqrt(variance + epsilon)
    scaled = centred * inv_std
    return (scaled * norm_gain + norm_bias, scaled, inv_std)


def norm_back(upstream, scaled, inv_std):
    mean_up = jnp.mean(upstream, axis=-1, keepdims=True)
    mean_cross = jnp.mean(upstream * scaled, axis=-1, keepdims=True)
    return inv_std * (upstream - mean_up - scaled * mean_cross)


def gelu_parts(pre_act):
    normal_cdf = 0.5 * (1.0 + lax.erf(pre_act * 0.7071067811865476))
    density = jnp.exp(-0.5 * pre_act * pre_act) * 0.3989422804014327
    return (pre_act * normal_cdf, normal_cdf + pre_act * density)


def encode(enc_input, enc_params):
    (
        mlp_gain,
        mlp_bias,
        fc1_weight,
        fc1_bias,
        fc2_weight,
        fc2_bias,
        encoder_gain,
        encoder_bias,
        embed_weight,
        embed_bias,
    ) = enc_params
    rows_in = enc_input.astype(jnp.float32)
    mlp_in, mlp_scaled, mlp_inv = layer_norm(rows_in, mlp_gain, mlp_bias)
    mlp_in = mlp_in.astype(jnp.bfloat16)
    pre_act = jnp.dot(mlp_in, fc1_weight, preferred_element_type=jnp.float32) + fc1_bias
    activation, slope = gelu_parts(pre_act)
    hidden = activation.astype(jnp.bfloat16)
    encoded = rows_in + jnp.dot(hidden, fc2_weight, preferred_element_type=jnp.float32) + fc2_bias
    normed, enc_scaled, enc_inv = layer_norm(encoded, encoder_gain, encoder_bias)
    normed = normed.astype(jnp.bfloat16)
    projected = (
        jnp.dot(normed, embed_weight, preferred_element_type=jnp.float32) + embed_bias
    ).astype(jnp.bfloat16)
    saved = (mlp_in, mlp_scaled, mlp_inv, slope, hidden, enc_scaled, enc_inv)
    return (saved, projected)


def encode_back(saved, grad_compact, enc_params):
    (
        mlp_gain,
        mlp_bias,
        fc1_weight,
        fc1_bias,
        fc2_weight,
        fc2_bias,
        encoder_gain,
        encoder_bias,
        embed_weight,
        embed_bias,
    ) = enc_params
    mlp_in, mlp_scaled, mlp_inv, slope, hidden, enc_scaled, enc_inv = saved
    grad_normed = jnp.dot(grad_compact, embed_weight.T, preferred_element_type=jnp.float32)
    grad_encoded = norm_back(grad_normed * encoder_gain, enc_scaled, enc_inv).astype(jnp.bfloat16)
    grad_hidden = jnp.dot(grad_encoded, fc2_weight.T, preferred_element_type=jnp.float32)
    grad_pre = (grad_hidden * slope).astype(jnp.bfloat16)
    grad_mlp_in = jnp.dot(grad_pre, fc1_weight.T, preferred_element_type=jnp.float32)
    grad_feats = (
        grad_encoded.astype(jnp.float32) + norm_back(grad_mlp_in * mlp_gain, mlp_scaled, mlp_inv)
    ).astype(jnp.bfloat16)
    return (mlp_in, grad_pre, hidden, grad_encoded, grad_feats)


def decoder_pass(
    projected_rows,
    keep_rows,
    position_ids,
    upstream,
    position_table,
    mask_token,
    decoder_gain,
    decoder_bias,
):
    table_ids = jnp.arange(position_table.shape[0], dtype=jnp.int32)[None, :]
    pick = (position_ids[:, None] == table_ids).astype(jnp.bfloat16)
    placed = jnp.dot(pick, position_table, preferred_element_type=jnp.float32)
    dec_input = jnp.where(keep_rows, projected_rows, mask_token) + placed
    decoded, dec_scaled, dec_inv = layer_norm(dec_input, decoder_gain, decoder_bias)
    grad_input = norm_back(upstream.astype(jnp.float32) * decoder_gain, dec_scaled, dec_inv)
    grad_projected = jnp.where(keep_rows, grad_input, 0.0).astype(jnp.bfloat16)
    return (decoded.astype(jnp.bfloat16), grad_projected)


def reduce_kernel(
    chunks,
    z_count,
    lhs_a,
    rhs_a,
    lhs_b,
    rhs_b,
    out_a,
    out_b,
    acc_a,
    acc_b,
    send0_a,
    send0_b,
    land0_a,
    land0_b,
    send1_a,
    send1_b,
    land1_a,
    land1_b,
    send2_a,
    send2_b,
    land2_a,
    land2_b,
    send3_a,
    send3_b,
    land3_a,
    land3_b,
    pair_sems,
    z_sems,
    spread_sems,
):
    dp = lax.axis_index("dp")
    tile = lax.axis_index("tile")
    x = lax.rem(dp, 2)
    y = lax.div(dp, 2)
    core = lax.rem(tile, 2)
    my_z = lax.div(tile, 2)
    sibling = (dp, tile + 1 - 2 * core)
    across_x = (dp + 1 - 2 * x, tile)
    across_y = (dp + 2 - 4 * y, tile)
    diagonal = (3 - dp, tile)
    z_to = [lax.rem(my_z + k, z_count) for k in range(1, z_count)]
    peers = [sibling, across_x, across_y, diagonal]
    peers += [(dp, 2 * z + core) for z in z_to]

    barrier = pltpu.get_barrier_semaphore()
    for peer in peers:
        pl.semaphore_signal(barrier, inc=1, device_id=peer, device_id_type=MESH)
    pl.semaphore_wait(barrier, len(peers))

    tensors = (
        (lhs_a, rhs_a, out_a, acc_a, send0_a, land0_a, send1_a, land1_a, send2_a, land2_a,
         send3_a, land3_a, x, y, across_x, across_y),
        (lhs_b, rhs_b, out_b, acc_b, send0_b, land0_b, send1_b, land1_b, send2_b, land2_b,
         send3_b, land3_b, y, x, across_y, across_x),
    )
    copies = {}

    def send(key, src, dst, sems, at, peer):
        copy = pltpu.make_async_remote_copy(
            src_ref=src,
            dst_ref=dst,
            send_sem=sems.at[(0,) + at],
            recv_sem=sems.at[(1,) + at],
            device_id=peer,
            device_id_type=MESH,
        )
        copy.start()
        copies[key] = copy

    def products(t, j, which, store):
        lhs, rhs = tensors[t][0], tensors[t][1]
        if t == 0:
            m = lhs.shape[2] // z_count

            @pl.loop(0, 4)
            def _(e):
                part = jnp.dot(lhs[j, which], rhs[e], preferred_element_type=jnp.float32)
                for z in range(z_count):
                    store(lax.div(e, 2), lax.rem(e, 2), z, part[z * m : (z + 1) * m])
        else:
            m = lhs.shape[3] // z_count

            @pl.loop(0, 4)
            def _(e):
                part = jnp.dot(lhs[j, which, e], rhs[...], preferred_element_type=jnp.float32)
                for z in range(z_count):
                    store(lax.div(e, 2), lax.rem(e, 2), z, part[z * m : (z + 1) * m])

    def stage0(t, j):
        acc, send0, land0 = tensors[t][3:6]

        def store_send(f, g, z, value):
            send0[j, f, g, z] = value.astype(jnp.bfloat16)

        def store_own(f, g, z, value):
            acc[j, f, g, z] = value

        products(t, j, 1 - core, store_send)
        send(("c", t, j), send0.at[j], land0.at[j], pair_sems, (0, t, j), sibling)
        products(t, j, core, store_own)

    def stage1(t, j):
        acc, _, land0, send1, land1 = tensors[t][3:8]
        f, partner = tensors[t][12], tensors[t][14]
        copies["c", t, j].wait()

        @pl.loop(0, z_count)
        def _(z):
            for g in range(2):
                send1[j, g, z] = (
                    acc[j, 1 - f, g, z] + land0[j, 1 - f, g, z].astype(jnp.float32)
                ).astype(jnp.bfloat16)

        send(("f", t, j), send1.at[j], land1.at[j], pair_sems, (1, t, j), partner)

        @pl.loop(0, z_count)
        def _(z):
            for g in range(2):
                acc[j, f, g, z] = acc[j, f, g, z] + land0[j, f, g, z].astype(jnp.float32)

    def stage2(t, j):
        acc = tensors[t][3]
        land1, send2, land2 = tensors[t][7:10]
        f, g, partner = tensors[t][12], tensors[t][13], tensors[t][15]
        copies["f", t, j].wait()

        @pl.loop(0, z_count)
        def _(z):
            send2[j, z] = (
                acc[j, f, 1 - g, z] + land1[j, 1 - g, z].astype(jnp.float32)
            ).astype(jnp.bfloat16)

        send(("g", t, j), send2.at[j], land2.at[j], pair_sems, (2, t, j), partner)

        @pl.loop(0, z_count)
        def _(z):
            acc[j, f, g, z] = acc[j, f, g, z] + land1[j, g, z].astype(jnp.float32)

    def stage3(t, j):
        acc = tensors[t][3]
        land2, send3, land3 = tensors[t][9:12]
        f, g = tensors[t][12], tensors[t][13]
        copies["g", t, j].wait()
        for k, z in enumerate(z_to):
            send3[j, k] = (acc[j, f, g, z] + land2[j, z].astype(jnp.float32)).astype(jnp.bfloat16)
            send(
                ("z", t, j, k), send3.at[j, k], land3.at[j, k], z_sems, (t, j, k),
                (dp, 2 * z + core),
            )
        acc[j, f, g, my_z] = acc[j, f, g, my_z] + land2[j, my_z].astype(jnp.float32)

    def stage4(t, j):
        out, acc = tensors[t][2:4]
        land3 = tensors[t][11]
        f, g = tensors[t][12], tensors[t][13]
        total = acc[j, f, g, my_z]
        for k in range(z_count - 1):
            copies["z", t, j, k].wait()
            total = total + land3[j, k].astype(jnp.float32)
        mine = 2 * f + g
        out[mine, j] = total.astype(jnp.bfloat16)
        for k, peer in enumerate((across_x, across_y, diagonal)):
            send(
                ("s", t, j, k), out.at[mine, j], out.at[mine, j], spread_sems, (t, j, k), peer
            )

    stages = (stage0, stage1, stage2, stage3, stage4)
    for step in range(chunks + len(stages) - 1):
        for at in reversed(range(len(stages))):
            j = step - at
            if 0 <= j < chunks:
                for t in range(2):
                    stages[at](t, j)
    for j in range(chunks):
        for t in range(2):
            for k in range(3):
                copies["s", t, j, k].wait()


def reduce_weights(mlp_in, grad_pre, hidden, grad_encoded, tiles):
    rows, width = mlp_in.shape
    inner = hidden.shape[1]
    z_count = tiles // 2
    rows_a, rows_b = width // tiles, inner // tiles // 4
    chunks = 5
    m_a, n_a = rows_a // chunks, inner // 4
    m_b, n_b = rows_b // chunks, width
    lhs_a = mlp_in.T.reshape(z_count, 2, chunks, m_a, rows).transpose(2, 1, 0, 3, 4)
    lhs_a = lhs_a.reshape(chunks, 2, z_count * m_a, rows)
    rhs_a = grad_pre.reshape(rows, 4, n_a).transpose(1, 0, 2)
    lhs_b = hidden.T.reshape(z_count, 2, 4, chunks, m_b, rows).transpose(3, 1, 2, 0, 4, 5)
    lhs_b = lhs_b.reshape(chunks, 2, 4, z_count * m_b, rows)
    whole = pl.BlockSpec(memory_space=pltpu.VMEM)
    half, full = jnp.bfloat16, jnp.float32
    scratch = []
    for lead, kind in (
        ((2, 2, z_count), full),
        ((2, 2, z_count), half),
        ((2, 2, z_count), half),
        ((2, z_count), half),
        ((2, z_count), half),
        ((z_count,), half),
        ((z_count,), half),
        ((z_count - 1,), half),
        ((z_count - 1,), half),
    ):
        for m, n in ((m_a, n_a), (m_b, n_b)):
            scratch.append(pltpu.VMEM((chunks,) + lead + (m, n), kind))
    scratch += [
        pltpu.SemaphoreType.DMA((2, 3, 2, chunks)),
        pltpu.SemaphoreType.DMA((2, 2, chunks, z_count - 1)),
        pltpu.SemaphoreType.DMA((2, 2, chunks, 3)),
    ]
    out_a, out_b = pl.pallas_call(
        functools.partial(reduce_kernel, chunks, z_count),
        out_shape=(
            jax.ShapeDtypeStruct((4, chunks, m_a, n_a), half),
            jax.ShapeDtypeStruct((4, chunks, m_b, n_b), half),
        ),
        in_specs=[whole] * 4,
        out_specs=(whole, whole),
        scratch_shapes=scratch,
        compiler_params=pltpu.CompilerParams(
            collective_id=0, has_side_effects=True, vmem_limit_bytes=56 * 2**20
        ),
    )(lhs_a, rhs_a, lhs_b, grad_encoded)
    fc1 = out_a.reshape(4, rows_a, n_a).transpose(1, 0, 2).reshape(rows_a, inner)
    fc2 = out_b.reshape(4 * rows_b, n_b)
    return fc1.astype(full), fc2.astype(full)


def reducible(mlp_in, hidden, scenes, tiles):
    width, inner = mlp_in.shape[1], hidden.shape[1]
    return (
        scenes == 4
        and tiles % 2 == 0
        and width % (tiles * 5 * 16) == 0
        and inner % (tiles * 4 * 5 * 16) == 0
        and inner % (4 * 128) == 0
        and width % 128 == 0
    )


def shards(
    features,
    visible,
    positions,
    cotangent,
    mlp_gain,
    mlp_bias,
    fc1_weight,
    fc1_bias,
    fc2_weight,
    fc2_bias,
    encoder_gain,
    encoder_bias,
    embed_weight,
    embed_bias,
    mask_token,
    position_table,
    decoder_gain,
    decoder_bias,
):
    patch_count = features.shape[2]
    model_width = features.shape[3]
    dec_width = embed_weight.shape[1]
    most_rows = patch_count // 2
    flags = visible.reshape(patch_count)
    row_data = features.reshape(patch_count, model_width)
    keep_rows = (flags > 0)[:, None]
    upstream = cotangent.reshape(patch_count, dec_width)
    ids = jnp.arange(patch_count, dtype=jnp.int32)
    row_rank = jnp.sum(jnp.where(ids[None, :] < ids[:, None], flags[None, :], 0), axis=1)
    slots = jnp.arange(most_rows, dtype=jnp.int32)
    target = jnp.where(flags > 0, row_rank, -1)
    gather = (slots[:, None] == target[None, :]).astype(jnp.bfloat16)
    scatter = (target[:, None] == slots[None, :]).astype(jnp.bfloat16)
    enc_params = (
        mlp_gain,
        mlp_bias,
        fc1_weight,
        fc1_bias,
        fc2_weight,
        fc2_bias,
        encoder_gain,
        encoder_bias,
        embed_weight,
        embed_bias,
    )
    decoder_args = (position_table, mask_token, decoder_gain, decoder_bias)
    enc_input = jnp.dot(gather, row_data, preferred_element_type=jnp.bfloat16)
    saved, projected = encode(enc_input, enc_params)
    projected_rows = jnp.dot(scatter, projected, preferred_element_type=jnp.float32)
    decoded, grad_projected = decoder_pass(
        projected_rows, keep_rows, positions.reshape(-1), upstream, *decoder_args
    )
    grad_compact = jnp.dot(gather, grad_projected, preferred_element_type=jnp.bfloat16)
    mlp_in, grad_pre, hidden, grad_encoded, grad_feats = encode_back(
        saved, grad_compact, enc_params
    )
    grad_rows = jnp.dot(scatter, grad_feats, preferred_element_type=jnp.bfloat16)
    device_total = lax.axis_size("dp") * lax.axis_size("tile")
    tiles = lax.axis_size("tile")
    if reducible(mlp_in, hidden, lax.axis_size("dp"), tiles):
        totals = reduce_weights(mlp_in, grad_pre, hidden, grad_encoded, tiles)
    else:
        totals = []
        for left, right in ((mlp_in, grad_pre), (hidden, grad_encoded)):
            term = jnp.dot(left.T, right, preferred_element_type=jnp.float32)
            share = lax.psum_scatter(
                term.astype(jnp.bfloat16), "tile", scatter_dimension=0, tiled=True
            )
            totals.append(lax.psum(share, "dp").astype(jnp.float32))
    fc1_grad, fc2_grad = [total / device_total for total in totals]
    feature_grad = grad_rows.reshape(features.shape)
    decoded_out = decoded.reshape(cotangent.shape)
    return (feature_grad, decoded_out, fc1_grad, fc2_grad)


def solution(mesh):
    return jax.shard_map(
        shards,
        mesh=mesh,
        in_specs=(
            P("dp", "tile", None, None),
            P("dp", "tile", None),
            P("dp", "tile", None),
            P("dp", "tile", None, None),
            P(),
            P(),
            P(),
            P(),
            P(),
            P(),
            P(),
            P(),
            P(),
            P(),
            P(),
            P(),
            P(),
            P(),
        ),
        out_specs=(
            P("dp", "tile", None, None),
            P("dp", "tile", None, None),
            P("tile", None),
            P("tile", None),
        ),
        check_vma=False,
    )
```

```python
import functools

import jax
import jax.numpy as jnp
from jax import lax
from jax.experimental import pallas as pl
from jax.experimental.pallas import tpu as pltpu
from jax.sharding import PartitionSpec as P

MESH = pl.DeviceIdType.MESH

epsilon = 1e-06


def layer_norm(values, norm_gain, norm_bias):
    row_mean = jnp.mean(values, axis=-1, keepdims=True)
    centred = values - row_mean
    variance = jnp.mean(centred * centred, axis=-1, keepdims=True)
    inv_std = lax.rsqrt(variance + epsilon)
    scaled = centred * inv_std
    return (scaled * norm_gain + norm_bias, scaled, inv_std)


def norm_back(upstream, scaled, inv_std):
    mean_up = jnp.mean(upstream, axis=-1, keepdims=True)
    mean_cross = jnp.mean(upstream * scaled, axis=-1, keepdims=True)
    return inv_std * (upstream - mean_up - scaled * mean_cross)


def gelu_parts(pre_act):
    normal_cdf = 0.5 * (1.0 + lax.erf(pre_act * 0.7071067811865476))
    density = jnp.exp(-0.5 * pre_act * pre_act) * 0.3989422804014327
    return (pre_act * normal_cdf, normal_cdf + pre_act * density)


def encode(enc_input, enc_params):
    (
        mlp_gain,
        mlp_bias,
        fc1_weight,
        fc1_bias,
        fc2_weight,
        fc2_bias,
        encoder_gain,
        encoder_bias,
        embed_weight,
        embed_bias,
    ) = enc_params
    rows_in = enc_input.astype(jnp.float32)
    mlp_in, mlp_scaled, mlp_inv = layer_norm(rows_in, mlp_gain, mlp_bias)
    mlp_in = mlp_in.astype(jnp.bfloat16)
    pre_act = jnp.dot(mlp_in, fc1_weight, preferred_element_type=jnp.float32) + fc1_bias
    activation, slope = gelu_parts(pre_act)
    hidden = activation.astype(jnp.bfloat16)
    encoded = rows_in + jnp.dot(hidden, fc2_weight, preferred_element_type=jnp.float32) + fc2_bias
    normed, enc_scaled, enc_inv = layer_norm(encoded, encoder_gain, encoder_bias)
    normed = normed.astype(jnp.bfloat16)
    projected = (
        jnp.dot(normed, embed_weight, preferred_element_type=jnp.float32) + embed_bias
    ).astype(jnp.bfloat16)
    saved = (mlp_in, mlp_scaled, mlp_inv, slope, hidden, enc_scaled, enc_inv)
    return (saved, projected)


def encode_back(saved, grad_compact, enc_params):
    (
        mlp_gain,
        mlp_bias,
        fc1_weight,
        fc1_bias,
        fc2_weight,
        fc2_bias,
        encoder_gain,
        encoder_bias,
        embed_weight,
        embed_bias,
    ) = enc_params
    mlp_in, mlp_scaled, mlp_inv, slope, hidden, enc_scaled, enc_inv = saved
    grad_normed = jnp.dot(grad_compact, embed_weight.T, preferred_element_type=jnp.float32)
    grad_encoded = norm_back(grad_normed * encoder_gain, enc_scaled, enc_inv).astype(jnp.bfloat16)
    grad_hidden = jnp.dot(grad_encoded, fc2_weight.T, preferred_element_type=jnp.float32)
    grad_pre = (grad_hidden * slope).astype(jnp.bfloat16)
    grad_mlp_in = jnp.dot(grad_pre, fc1_weight.T, preferred_element_type=jnp.float32)
    grad_feats = (
        grad_encoded.astype(jnp.float32) + norm_back(grad_mlp_in * mlp_gain, mlp_scaled, mlp_inv)
    ).astype(jnp.bfloat16)
    return (mlp_in, grad_pre, hidden, grad_encoded, grad_feats)


def decoder_pass(
    projected_rows,
    keep_rows,
    position_ids,
    upstream,
    position_table,
    mask_token,
    decoder_gain,
    decoder_bias,
):
    table_ids = jnp.arange(position_table.shape[0], dtype=jnp.int32)[None, :]
    pick = (position_ids[:, None] == table_ids).astype(jnp.bfloat16)
    placed = jnp.dot(pick, position_table, preferred_element_type=jnp.float32)
    dec_input = jnp.where(keep_rows, projected_rows, mask_token) + placed
    decoded, dec_scaled, dec_inv = layer_norm(dec_input, decoder_gain, decoder_bias)
    grad_input = norm_back(upstream.astype(jnp.float32) * decoder_gain, dec_scaled, dec_inv)
    grad_projected = jnp.where(keep_rows, grad_input, 0.0).astype(jnp.bfloat16)
    return (decoded.astype(jnp.bfloat16), grad_projected)


def reduce_kernel(
    chunks,
    z_count,
    lhs_a,
    rhs_a,
    lhs_b,
    rhs_b,
    out_a,
    out_b,
    turned_a,
    turned_b,
    gathered_a,
    gathered_b,
    acc_a,
    acc_b,
    send0_a,
    send0_b,
    land0_a,
    land0_b,
    send1_a,
    send1_b,
    land1_a,
    land1_b,
    send2_a,
    send2_b,
    land2_a,
    land2_b,
    send3_a,
    send3_b,
    land3_a,
    land3_b,
    pair_sems,
    z_sems,
    spread_sems,
):
    dp = lax.axis_index("dp")
    tile = lax.axis_index("tile")
    x = lax.rem(dp, 2)
    y = lax.div(dp, 2)
    core = lax.rem(tile, 2)
    my_z = lax.div(tile, 2)
    sibling = (dp, tile + 1 - 2 * core)
    across_x = (dp + 1 - 2 * x, tile)
    across_y = (dp + 2 - 4 * y, tile)
    diagonal = (3 - dp, tile)
    z_to = [lax.rem(my_z + k, z_count) for k in range(1, z_count)]
    peers = [sibling, across_x, across_y, diagonal]
    peers += [(dp, 2 * z + core) for z in z_to]

    barrier = pltpu.get_barrier_semaphore()
    for peer in peers:
        pl.semaphore_signal(barrier, inc=1, device_id=peer, device_id_type=MESH)
    pl.semaphore_wait(barrier, len(peers))

    tensors = (
        (turned_a, rhs_a, gathered_a, acc_a, send0_a, land0_a, send1_a, land1_a, send2_a, land2_a,
         send3_a, land3_a, x, y, across_x, across_y),
        (turned_b, rhs_b, gathered_b, acc_b, send0_b, land0_b, send1_b, land1_b, send2_b, land2_b,
         send3_b, land3_b, y, x, across_y, across_x),
    )
    copies = {}

    def send(key, src, dst, sems, at, peer):
        copy = pltpu.make_async_remote_copy(
            src_ref=src,
            dst_ref=dst,
            send_sem=sems.at[(0,) + at],
            recv_sem=sems.at[(1,) + at],
            device_id=peer,
            device_id_type=MESH,
        )
        copy.start()
        copies[key] = copy

    def products(t, j, which, store):
        lhs, rhs = tensors[t][0], tensors[t][1]
        rows = lhs.shape[0] // (2 * z_count)
        columns = rhs.shape[1] // chunks

        @pl.loop(0, z_count)
        def _(z):
            first = pl.multiple_of((2 * z + which) * rows, 16)
            part = jnp.dot(
                lhs[pl.ds(first, rows), :],
                rhs[:, j * columns : (j + 1) * columns],
                preferred_element_type=jnp.float32,
            )
            for e in range(4):
                if t == 0:
                    width = columns // 4
                    store(e // 2, e % 2, z, part[:, e * width : (e + 1) * width])
                else:
                    store(e // 2, e % 2, z, part[e * (rows // 4) : (e + 1) * (rows // 4)])

    def stage0(t, j):
        acc, send0, land0 = tensors[t][3:6]

        def store_send(f, g, z, value):
            send0[j, f, g, z] = value.astype(jnp.bfloat16)

        def store_own(f, g, z, value):
            acc[j, f, g, z] = value

        if j == 0:
            source = (lhs_a, lhs_b)[t]
            for at in range(0, source.shape[1], 256):
                tensors[t][0][at : at + 256, :] = source[:, at : at + 256].T
        products(t, j, 1 - core, store_send)
        send(("c", t, j), send0.at[j], land0.at[j], pair_sems, (0, t, j), sibling)
        products(t, j, core, store_own)

    def stage1(t, j):
        acc, _, land0, send1, land1 = tensors[t][3:8]
        f, partner = tensors[t][12], tensors[t][14]
        copies["c", t, j].wait()

        @pl.loop(0, z_count)
        def _(z):
            for g in range(2):
                send1[j, g, z] = (
                    acc[j, 1 - f, g, z] + land0[j, 1 - f, g, z].astype(jnp.float32)
                ).astype(jnp.bfloat16)

        send(("f", t, j), send1.at[j], land1.at[j], pair_sems, (1, t, j), partner)

        @pl.loop(0, z_count)
        def _(z):
            for g in range(2):
                acc[j, f, g, z] = acc[j, f, g, z] + land0[j, f, g, z].astype(jnp.float32)

    def stage2(t, j):
        acc = tensors[t][3]
        land1, send2, land2 = tensors[t][7:10]
        f, g, partner = tensors[t][12], tensors[t][13], tensors[t][15]
        copies["f", t, j].wait()

        @pl.loop(0, z_count)
        def _(z):
            send2[j, z] = (
                acc[j, f, 1 - g, z] + land1[j, 1 - g, z].astype(jnp.float32)
            ).astype(jnp.bfloat16)

        send(("g", t, j), send2.at[j], land2.at[j], pair_sems, (2, t, j), partner)

        @pl.loop(0, z_count)
        def _(z):
            acc[j, f, g, z] = acc[j, f, g, z] + land1[j, g, z].astype(jnp.float32)

    def stage3(t, j):
        acc = tensors[t][3]
        land2, send3, land3 = tensors[t][9:12]
        f, g = tensors[t][12], tensors[t][13]
        copies["g", t, j].wait()
        for k, z in enumerate(z_to):
            send3[j, k] = (acc[j, f, g, z] + land2[j, z].astype(jnp.float32)).astype(jnp.bfloat16)
            send(
                ("z", t, j, k), send3.at[j, k], land3.at[j, k], z_sems, (t, j, k),
                (dp, 2 * z + core),
            )
        acc[j, f, g, my_z] = acc[j, f, g, my_z] + land2[j, my_z].astype(jnp.float32)

    def stage4(t, j):
        out, acc = tensors[t][2:4]
        land3 = tensors[t][11]
        f, g = tensors[t][12], tensors[t][13]
        total = acc[j, f, g, my_z]
        for k in range(z_count - 1):
            copies["z", t, j, k].wait()
            total = total + land3[j, k].astype(jnp.float32)
        mine = 2 * f + g
        out[mine, j] = total.astype(jnp.bfloat16)
        for k, peer in enumerate((across_x, across_y, diagonal)):
            send(
                ("s", t, j, k), out.at[mine, j], out.at[mine, j], spread_sems, (t, j, k), peer
            )

    def stage5(t, j):
        gathered = tensors[t][2]
        for k in range(3):
            copies["s", t, j, k].wait()
        m, n = gathered.shape[2:]
        for e in range(4):
            if t == 0:
                out_a[:, (4 * j + e) * n : (4 * j + e + 1) * n] = gathered[e, j]
            else:
                out_b[e * m : (e + 1) * m, j * n : (j + 1) * n] = gathered[e, j]

    stages = (stage0, stage1, stage2, stage3, stage4, stage5)
    for step in range(chunks + len(stages) - 1):
        for at in reversed(range(len(stages))):
            j = step - at
            if 0 <= j < chunks:
                for t in range(2):
                    stages[at](t, j)


def reduce_weights(mlp_in, grad_pre, hidden, grad_encoded, tiles):
    rows, width = mlp_in.shape
    inner = hidden.shape[1]
    z_count = tiles // 2
    rows_a, rows_b = width // tiles, inner // tiles // 4
    chunks = 5
    m_a, n_a = rows_a, inner // chunks // 4
    m_b, n_b = rows_b, width // chunks
    whole = pl.BlockSpec(memory_space=pltpu.VMEM)
    half, full = jnp.bfloat16, jnp.float32
    scratch = [
        pltpu.VMEM((width, rows), half),
        pltpu.VMEM((inner, rows), half),
        pltpu.VMEM((4, chunks, m_a, n_a), half),
        pltpu.VMEM((4, chunks, m_b, n_b), half),
    ]
    for lead, kind in (
        ((2, 2, z_count), full),
        ((2, 2, z_count), half),
        ((2, 2, z_count), half),
        ((2, z_count), half),
        ((2, z_count), half),
        ((z_count,), half),
        ((z_count,), half),
        ((z_count - 1,), half),
        ((z_count - 1,), half),
    ):
        for m, n in ((m_a, n_a), (m_b, n_b)):
            scratch.append(pltpu.VMEM((chunks,) + lead + (m, n), kind))
    scratch += [
        pltpu.SemaphoreType.DMA((2, 3, 2, chunks)),
        pltpu.SemaphoreType.DMA((2, 2, chunks, z_count - 1)),
        pltpu.SemaphoreType.DMA((2, 2, chunks, 3)),
    ]
    out_a, out_b = pl.pallas_call(
        functools.partial(reduce_kernel, chunks, z_count),
        out_shape=(
            jax.ShapeDtypeStruct((rows_a, inner), half),
            jax.ShapeDtypeStruct((4 * rows_b, width), half),
        ),
        in_specs=[whole] * 4,
        out_specs=(whole, whole),
        scratch_shapes=scratch,
        compiler_params=pltpu.CompilerParams(
            collective_id=0, has_side_effects=True, vmem_limit_bytes=56 * 2**20
        ),
    )(mlp_in, grad_pre, hidden, grad_encoded)
    return out_a.astype(full), out_b.astype(full)


def reducible(mlp_in, hidden, scenes, tiles):
    width, inner = mlp_in.shape[1], hidden.shape[1]
    return (
        scenes == 4
        and tiles % 2 == 0
        and width % (tiles * 16) == 0
        and inner % (tiles * 4 * 16) == 0
        and inner % (5 * 4 * 128) == 0
        and width % (5 * 128) == 0
    )


def shards(
    features,
    visible,
    positions,
    cotangent,
    mlp_gain,
    mlp_bias,
    fc1_weight,
    fc1_bias,
    fc2_weight,
    fc2_bias,
    encoder_gain,
    encoder_bias,
    embed_weight,
    embed_bias,
    mask_token,
    position_table,
    decoder_gain,
    decoder_bias,
):
    patch_count = features.shape[2]
    model_width = features.shape[3]
    dec_width = embed_weight.shape[1]
    most_rows = patch_count // 2
    flags = visible.reshape(patch_count)
    row_data = features.reshape(patch_count, model_width)
    keep_rows = (flags > 0)[:, None]
    upstream = cotangent.reshape(patch_count, dec_width)
    ids = jnp.arange(patch_count, dtype=jnp.int32)
    row_rank = jnp.sum(jnp.where(ids[None, :] < ids[:, None], flags[None, :], 0), axis=1)
    slots = jnp.arange(most_rows, dtype=jnp.int32)
    target = jnp.where(flags > 0, row_rank, -1)
    gather = (slots[:, None] == target[None, :]).astype(jnp.bfloat16)
    scatter = (target[:, None] == slots[None, :]).astype(jnp.bfloat16)
    enc_params = (
        mlp_gain,
        mlp_bias,
        fc1_weight,
        fc1_bias,
        fc2_weight,
        fc2_bias,
        encoder_gain,
        encoder_bias,
        embed_weight,
        embed_bias,
    )
    decoder_args = (position_table, mask_token, decoder_gain, decoder_bias)
    enc_input = jnp.dot(gather, row_data, preferred_element_type=jnp.bfloat16)
    saved, projected = encode(enc_input, enc_params)
    projected_rows = jnp.dot(scatter, projected, preferred_element_type=jnp.float32)
    decoded, grad_projected = decoder_pass(
        projected_rows, keep_rows, positions.reshape(-1), upstream, *decoder_args
    )
    grad_compact = jnp.dot(gather, grad_projected, preferred_element_type=jnp.bfloat16)
    mlp_in, grad_pre, hidden, grad_encoded, grad_feats = encode_back(
        saved, grad_compact, enc_params
    )
    grad_rows = jnp.dot(scatter, grad_feats, preferred_element_type=jnp.bfloat16)
    device_total = lax.axis_size("dp") * lax.axis_size("tile")
    tiles = lax.axis_size("tile")
    if reducible(mlp_in, hidden, lax.axis_size("dp"), tiles):
        totals = reduce_weights(mlp_in, grad_pre, hidden, grad_encoded, tiles)
    else:
        totals = []
        for left, right in ((mlp_in, grad_pre), (hidden, grad_encoded)):
            term = jnp.dot(left.T, right, preferred_element_type=jnp.float32)
            share = lax.psum_scatter(
                term.astype(jnp.bfloat16), "tile", scatter_dimension=0, tiled=True
            )
            totals.append(lax.psum(share, "dp").astype(jnp.float32))
    fc1_grad, fc2_grad = [total / device_total for total in totals]
    feature_grad = grad_rows.reshape(features.shape)
    decoded_out = decoded.reshape(cotangent.shape)
    return (feature_grad, decoded_out, fc1_grad, fc2_grad)


def solution(mesh):
    return jax.shard_map(
        shards,
        mesh=mesh,
        in_specs=(
            P("dp", "tile", None, None),
            P("dp", "tile", None),
            P("dp", "tile", None),
            P("dp", "tile", None, None),
            P(),
            P(),
            P(),
            P(),
            P(),
            P(),
            P(),
            P(),
            P(),
            P(),
            P(),
            P(),
            P(),
            P(),
        ),
        out_specs=(
            P("dp", "tile", None, None),
            P("dp", "tile", None, None),
            P("tile", None),
            P("tile", None),
        ),
        check_vma=False,
    )
```

```python
import functools

import jax
import jax.numpy as jnp
from jax import lax
from jax.experimental import pallas as pl
from jax.experimental.pallas import tpu as pltpu
from jax.sharding import PartitionSpec as P

MESH = pl.DeviceIdType.MESH

epsilon = 1e-06


def layer_norm(values, norm_gain, norm_bias):
    row_mean = jnp.mean(values, axis=-1, keepdims=True)
    centred = values - row_mean
    variance = jnp.mean(centred * centred, axis=-1, keepdims=True)
    inv_std = lax.rsqrt(variance + epsilon)
    scaled = centred * inv_std
    return (scaled * norm_gain + norm_bias, scaled, inv_std)


def norm_back(upstream, scaled, inv_std):
    mean_up = jnp.mean(upstream, axis=-1, keepdims=True)
    mean_cross = jnp.mean(upstream * scaled, axis=-1, keepdims=True)
    return inv_std * (upstream - mean_up - scaled * mean_cross)


def gelu_parts(pre_act):
    normal_cdf = 0.5 * (1.0 + lax.erf(pre_act * 0.7071067811865476))
    density = jnp.exp(-0.5 * pre_act * pre_act) * 0.3989422804014327
    return (pre_act * normal_cdf, normal_cdf + pre_act * density)


def encode(enc_input, enc_params):
    (
        mlp_gain,
        mlp_bias,
        fc1_weight,
        fc1_bias,
        fc2_weight,
        fc2_bias,
        encoder_gain,
        encoder_bias,
        embed_weight,
        embed_bias,
    ) = enc_params
    rows_in = enc_input.astype(jnp.float32)
    mlp_in, mlp_scaled, mlp_inv = layer_norm(rows_in, mlp_gain, mlp_bias)
    mlp_in = mlp_in.astype(jnp.bfloat16)
    pre_act = jnp.dot(mlp_in, fc1_weight, preferred_element_type=jnp.float32) + fc1_bias
    activation, slope = gelu_parts(pre_act)
    hidden = activation.astype(jnp.bfloat16)
    encoded = rows_in + jnp.dot(hidden, fc2_weight, preferred_element_type=jnp.float32) + fc2_bias
    normed, enc_scaled, enc_inv = layer_norm(encoded, encoder_gain, encoder_bias)
    normed = normed.astype(jnp.bfloat16)
    projected = (
        jnp.dot(normed, embed_weight, preferred_element_type=jnp.float32) + embed_bias
    ).astype(jnp.bfloat16)
    saved = (mlp_in, mlp_scaled, mlp_inv, slope, hidden, enc_scaled, enc_inv)
    return (saved, projected)


def encode_back(saved, grad_compact, enc_params):
    (
        mlp_gain,
        mlp_bias,
        fc1_weight,
        fc1_bias,
        fc2_weight,
        fc2_bias,
        encoder_gain,
        encoder_bias,
        embed_weight,
        embed_bias,
    ) = enc_params
    mlp_in, mlp_scaled, mlp_inv, slope, hidden, enc_scaled, enc_inv = saved
    grad_normed = jnp.dot(grad_compact, embed_weight.T, preferred_element_type=jnp.float32)
    grad_encoded = norm_back(grad_normed * encoder_gain, enc_scaled, enc_inv).astype(jnp.bfloat16)
    grad_hidden = jnp.dot(grad_encoded, fc2_weight.T, preferred_element_type=jnp.float32)
    grad_pre = (grad_hidden * slope).astype(jnp.bfloat16)
    grad_mlp_in = jnp.dot(grad_pre, fc1_weight.T, preferred_element_type=jnp.float32)
    grad_feats = (
        grad_encoded.astype(jnp.float32) + norm_back(grad_mlp_in * mlp_gain, mlp_scaled, mlp_inv)
    ).astype(jnp.bfloat16)
    return (mlp_in, grad_pre, hidden, grad_encoded, grad_feats)


def decoder_pass(
    projected_rows,
    keep_rows,
    position_ids,
    upstream,
    position_table,
    mask_token,
    decoder_gain,
    decoder_bias,
):
    table_ids = jnp.arange(position_table.shape[0], dtype=jnp.int32)[None, :]
    pick = (position_ids[:, None] == table_ids).astype(jnp.bfloat16)
    placed = jnp.dot(pick, position_table, preferred_element_type=jnp.float32)
    dec_input = jnp.where(keep_rows, projected_rows, mask_token) + placed
    decoded, dec_scaled, dec_inv = layer_norm(dec_input, decoder_gain, decoder_bias)
    grad_input = norm_back(upstream.astype(jnp.float32) * decoder_gain, dec_scaled, dec_inv)
    grad_projected = jnp.where(keep_rows, grad_input, 0.0).astype(jnp.bfloat16)
    return (decoded.astype(jnp.bfloat16), grad_projected)


def reduce_kernel(
    chunks,
    z_count,
    lhs_a,
    rhs_a,
    lhs_b,
    rhs_b,
    weight,
    gain,
    scaled,
    inverse,
    scatter,
    out_a,
    out_b,
    feature_out,
    weight_held,
    upstream,
    grad_rows,
    turned_a,
    turned_b,
    gathered_a,
    gathered_b,
    acc_a,
    acc_b,
    send0_a,
    send0_b,
    land0_a,
    land0_b,
    land1_a,
    land1_b,
    land2_a,
    land2_b,
    land3_a,
    land3_b,
    pair_sems,
    z_sems,
    spread_sems,
    weight_sem,
):
    dp = lax.axis_index("dp")
    tile = lax.axis_index("tile")
    x = lax.rem(dp, 2)
    y = lax.div(dp, 2)
    core = lax.rem(tile, 2)
    my_z = lax.div(tile, 2)
    sibling = (dp, tile + 1 - 2 * core)
    across_x = (dp + 1 - 2 * x, tile)
    across_y = (dp + 2 - 4 * y, tile)
    diagonal = (3 - dp, tile)
    z_to = [lax.rem(my_z + k, z_count) for k in range(1, z_count)]
    peers = [sibling, across_x, across_y, diagonal]
    peers += [(dp, 2 * z + core) for z in z_to]

    fetch = pltpu.make_async_copy(weight, weight_held, weight_sem)
    fetch.start()
    barrier = pltpu.get_barrier_semaphore()
    for peer in peers:
        pl.semaphore_signal(barrier, inc=1, device_id=peer, device_id_type=MESH)
    pl.semaphore_wait(barrier, len(peers))

    tensors = (
        (turned_a, rhs_a, gathered_a, acc_a, send0_a, land0_a, send0_a, land1_a, send0_a, land2_a,
         send0_a, land3_a, x, y, across_x, across_y),
        (turned_b, rhs_b, gathered_b, acc_b, send0_b, land0_b, send0_b, land1_b, send0_b, land2_b,
         send0_b, land3_b, y, x, across_y, across_x),
    )
    copies = {}

    def send(key, src, dst, sems, at, peer):
        copy = pltpu.make_async_remote_copy(
            src_ref=src,
            dst_ref=dst,
            send_sem=sems.at[(0,) + at],
            recv_sem=sems.at[(1,) + at],
            device_id=peer,
            device_id_type=MESH,
        )
        copy.start()
        copies[key] = copy

    def products(t, j, which, store):
        lhs, rhs = tensors[t][0], tensors[t][1]
        rows = lhs.shape[0] // (2 * z_count)
        columns = rhs.shape[1] // chunks

        @pl.loop(0, z_count)
        def _(z):
            first = pl.multiple_of((2 * z + which) * rows, 16)
            part = jnp.dot(
                lhs[pl.ds(first, rows), :],
                rhs[:, j * columns : (j + 1) * columns],
                preferred_element_type=jnp.float32,
            )
            for e in range(4):
                if t == 0:
                    width = columns // 4
                    store(e // 2, e % 2, z, part[:, e * width : (e + 1) * width])
                else:
                    store(e // 2, e % 2, z, part[e * (rows // 4) : (e + 1) * (rows // 4)])

    def stage0(t, j):
        acc, send0, land0 = tensors[t][3:6]

        def store_send(f, g, z, value):
            send0[j, f, g, z] = value.astype(jnp.bfloat16)

        def store_own(f, g, z, value):
            acc[j, f, g, z] = value

        if j == 0:
            source = (lhs_a, lhs_b)[t]
            for at in range(0, source.shape[1], 256):
                tensors[t][0][at : at + 256, :] = source[:, at : at + 256].T
        products(t, j, 1 - core, store_send)
        send(("c", t, j), send0.at[j], land0.at[j], pair_sems, (0, t, j), sibling)
        products(t, j, core, store_own)

    def stage1(t, j):
        acc, _, land0, send1, land1 = tensors[t][3:8]
        f, partner = tensors[t][12], tensors[t][14]
        copies["c", t, j].wait()

        @pl.loop(0, z_count)
        def _(z):
            for g in range(2):
                send1[j, 0, g, z] = (
                    acc[j, 1 - f, g, z] + land0[j, 1 - f, g, z].astype(jnp.float32)
                ).astype(jnp.bfloat16)

        send(("f", t, j), send1.at[j, 0], land1.at[j], pair_sems, (1, t, j), partner)

        @pl.loop(0, z_count)
        def _(z):
            for g in range(2):
                acc[j, f, g, z] = acc[j, f, g, z] + land0[j, f, g, z].astype(jnp.float32)

    def stage2(t, j):
        acc = tensors[t][3]
        land1, send2, land2 = tensors[t][7:10]
        f, g, partner = tensors[t][12], tensors[t][13], tensors[t][15]
        copies["f", t, j].wait()

        @pl.loop(0, z_count)
        def _(z):
            send2[j, 1, 0, z] = (
                acc[j, f, 1 - g, z] + land1[j, 1 - g, z].astype(jnp.float32)
            ).astype(jnp.bfloat16)

        send(("g", t, j), send2.at[j, 1, 0], land2.at[j], pair_sems, (2, t, j), partner)

        @pl.loop(0, z_count)
        def _(z):
            acc[j, f, g, z] = acc[j, f, g, z] + land1[j, g, z].astype(jnp.float32)

    def stage3(t, j):
        acc = tensors[t][3]
        land2, send3, land3 = tensors[t][9:12]
        f, g = tensors[t][12], tensors[t][13]
        copies["g", t, j].wait()
        for k, z in enumerate(z_to):
            send3[j, 1, 1, k] = (acc[j, f, g, z] + land2[j, z].astype(jnp.float32)).astype(jnp.bfloat16)
            send(
                ("z", t, j, k), send3.at[j, 1, 1, k], land3.at[j, k], z_sems, (t, j, k),
                (dp, 2 * z + core),
            )
        acc[j, f, g, my_z] = acc[j, f, g, my_z] + land2[j, my_z].astype(jnp.float32)

    def stage4(t, j):
        out, acc = tensors[t][2:4]
        land3 = tensors[t][11]
        f, g = tensors[t][12], tensors[t][13]
        total = acc[j, f, g, my_z]
        for k in range(z_count - 1):
            copies["z", t, j, k].wait()
            total = total + land3[j, k].astype(jnp.float32)
        mine = 2 * f + g
        out[mine, j] = total.astype(jnp.bfloat16)
        for k, peer in enumerate((across_x, across_y, diagonal)):
            send(
                ("s", t, j, k), out.at[mine, j], out.at[mine, j], spread_sems, (t, j, k), peer
            )

    def stage5(t, j):
        gathered = tensors[t][2]
        for k in range(3):
            copies["s", t, j, k].wait()
        m, n = gathered.shape[2:]
        for e in range(4):
            if t == 0:
                out_a[:, (4 * j + e) * n : (4 * j + e + 1) * n] = gathered[e, j]
            else:
                out_b[e * m : (e + 1) * m, j * n : (j + 1) * n] = gathered[e, j]

    def feature_columns(q):
        if q == 0:
            fetch.wait()
        wide = weight_held.shape[0] // chunks
        at = slice(q * wide, (q + 1) * wide)
        part = lax.dot_general(
            rhs_a[...],
            weight_held[at, :],
            (((1,), (1,)), ((), ())),
            preferred_element_type=jnp.float32,
        )
        upstream[:, at] = part * gain[:, at]

    def feature_rows():
        block = upstream.shape[0] // 8

        @pl.loop(0, 8)
        def _(i):
            at = pl.ds(pl.multiple_of(i * block, block), block)
            back = norm_back(upstream[at, :], scaled[at, :], inverse[at, :])
            grad_rows[at, :] = (rhs_b[at, :].astype(jnp.float32) + back).astype(jnp.bfloat16)

        tall = feature_out.shape[0] // 4

        @pl.loop(0, 4)
        def _(i):
            at = pl.ds(pl.multiple_of(i * tall, tall), tall)
            feature_out[at, :] = jnp.dot(
                scatter[at, :], grad_rows[...], preferred_element_type=jnp.float32
            ).astype(jnp.bfloat16)

    stages = (stage0, stage1, stage2, stage3, stage4, stage5)
    for step in range(chunks + len(stages) - 1):
        for at in reversed(range(len(stages))):
            j = step - at
            if 0 <= j < chunks:
                for t in range(2):
                    stages[at](t, j)
        if 1 <= step <= chunks:
            feature_columns(step - 1)
        if step == chunks + 1:
            feature_rows()


def reduce_weights(
    mlp_in, grad_pre, hidden, grad_encoded, tiles, fc1_weight, mlp_gain, mlp_scaled, mlp_inv, scatter
):
    rows, width = mlp_in.shape
    inner = hidden.shape[1]
    z_count = tiles // 2
    rows_a, rows_b = width // tiles, inner // tiles // 4
    chunks = 5
    m_a, n_a = rows_a, inner // chunks // 4
    m_b, n_b = rows_b, width // chunks
    whole = pl.BlockSpec(memory_space=pltpu.VMEM)
    half, full = jnp.bfloat16, jnp.float32
    scratch = [
        pltpu.VMEM((width, inner), half),
        pltpu.VMEM((rows, width), full),
        pltpu.VMEM((rows, width), half),
        pltpu.VMEM((width, rows), half),
        pltpu.VMEM((inner, rows), half),
        pltpu.VMEM((4, chunks, m_a, n_a), half),
        pltpu.VMEM((4, chunks, m_b, n_b), half),
    ]
    for lead, kind in (
        ((2, 2, z_count), full),
        ((2, 2, z_count), half),
        ((2, 2, z_count), half),
        ((2, z_count), half),
        ((z_count,), half),
        ((z_count - 1,), half),
    ):
        for m, n in ((m_a, n_a), (m_b, n_b)):
            scratch.append(pltpu.VMEM((chunks,) + lead + (m, n), kind))
    scratch += [
        pltpu.SemaphoreType.DMA((2, 3, 2, chunks)),
        pltpu.SemaphoreType.DMA((2, 2, chunks, z_count - 1)),
        pltpu.SemaphoreType.DMA((2, 2, chunks, 3)),
        pltpu.SemaphoreType.DMA,
    ]
    out_a, out_b, features = pl.pallas_call(
        functools.partial(reduce_kernel, chunks, z_count),
        out_shape=(
            jax.ShapeDtypeStruct((rows_a, inner), half),
            jax.ShapeDtypeStruct((4 * rows_b, width), half),
            jax.ShapeDtypeStruct((scatter.shape[0], width), half),
        ),
        in_specs=[whole] * 4 + [pl.BlockSpec(memory_space=pl.ANY)] + [whole] * 4,
        out_specs=(whole, whole, whole),
        scratch_shapes=scratch,
        compiler_params=pltpu.CompilerParams(
            collective_id=0, has_side_effects=True, vmem_limit_bytes=56 * 2**20
        ),
    )(
        mlp_in,
        grad_pre,
        hidden,
        grad_encoded,
        fc1_weight,
        mlp_gain[None, :],
        mlp_scaled,
        mlp_inv,
        scatter,
    )
    return (out_a.astype(full), out_b.astype(full)), features


def reducible(mlp_in, hidden, scenes, tiles):
    width, inner = mlp_in.shape[1], hidden.shape[1]
    return (
        scenes == 4
        and tiles % 2 == 0
        and width % (tiles * 16) == 0
        and inner % (tiles * 4 * 16) == 0
        and inner % (5 * 4 * 128) == 0
        and width % (5 * 128) == 0
    )


def shards(
    features,
    visible,
    positions,
    cotangent,
    mlp_gain,
    mlp_bias,
    fc1_weight,
    fc1_bias,
    fc2_weight,
    fc2_bias,
    encoder_gain,
    encoder_bias,
    embed_weight,
    embed_bias,
    mask_token,
    position_table,
    decoder_gain,
    decoder_bias,
):
    patch_count = features.shape[2]
    model_width = features.shape[3]
    dec_width = embed_weight.shape[1]
    most_rows = patch_count // 2
    flags = visible.reshape(patch_count)
    row_data = features.reshape(patch_count, model_width)
    keep_rows = (flags > 0)[:, None]
    upstream = cotangent.reshape(patch_count, dec_width)
    ids = jnp.arange(patch_count, dtype=jnp.int32)
    row_rank = jnp.sum(jnp.where(ids[None, :] < ids[:, None], flags[None, :], 0), axis=1)
    slots = jnp.arange(most_rows, dtype=jnp.int32)
    target = jnp.where(flags > 0, row_rank, -1)
    gather = (slots[:, None] == target[None, :]).astype(jnp.bfloat16)
    scatter = (target[:, None] == slots[None, :]).astype(jnp.bfloat16)
    enc_params = (
        mlp_gain,
        mlp_bias,
        fc1_weight,
        fc1_bias,
        fc2_weight,
        fc2_bias,
        encoder_gain,
        encoder_bias,
        embed_weight,
        embed_bias,
    )
    decoder_args = (position_table, mask_token, decoder_gain, decoder_bias)
    enc_input = jnp.dot(gather, row_data, preferred_element_type=jnp.bfloat16)
    saved, projected = encode(enc_input, enc_params)
    projected_rows = jnp.dot(scatter, projected, preferred_element_type=jnp.float32)
    decoded, grad_projected = decoder_pass(
        projected_rows, keep_rows, positions.reshape(-1), upstream, *decoder_args
    )
    grad_compact = jnp.dot(gather, grad_projected, preferred_element_type=jnp.bfloat16)
    mlp_in, grad_pre, hidden, grad_encoded, grad_feats = encode_back(
        saved, grad_compact, enc_params
    )
    device_total = lax.axis_size("dp") * lax.axis_size("tile")
    tiles = lax.axis_size("tile")
    if reducible(mlp_in, hidden, lax.axis_size("dp"), tiles):
        totals, grad_rows = reduce_weights(
            mlp_in,
            grad_pre,
            hidden,
            grad_encoded,
            tiles,
            fc1_weight,
            mlp_gain,
            saved[1],
            saved[2],
            scatter,
        )
    else:
        grad_rows = jnp.dot(scatter, grad_feats, preferred_element_type=jnp.bfloat16)
        totals = []
        for left, right in ((mlp_in, grad_pre), (hidden, grad_encoded)):
            term = jnp.dot(left.T, right, preferred_element_type=jnp.float32)
            share = lax.psum_scatter(
                term.astype(jnp.bfloat16), "tile", scatter_dimension=0, tiled=True
            )
            totals.append(lax.psum(share, "dp").astype(jnp.float32))
    fc1_grad, fc2_grad = [total / device_total for total in totals]
    feature_grad = grad_rows.reshape(features.shape)
    decoded_out = decoded.reshape(cotangent.shape)
    return (feature_grad, decoded_out, fc1_grad, fc2_grad)


def solution(mesh):
    return jax.shard_map(
        shards,
        mesh=mesh,
        in_specs=(
            P("dp", "tile", None, None),
            P("dp", "tile", None),
            P("dp", "tile", None),
            P("dp", "tile", None, None),
            P(),
            P(),
            P(),
            P(),
            P(),
            P(),
            P(),
            P(),
            P(),
            P(),
            P(),
            P(),
            P(),
            P(),
        ),
        out_specs=(
            P("dp", "tile", None, None),
            P("dp", "tile", None, None),
            P("tile", None),
            P("tile", None),
        ),
        check_vma=False,
    )
```

```python
import functools

import jax
import jax.numpy as jnp
from jax import lax
from jax.experimental import pallas as pl
from jax.experimental.pallas import tpu as pltpu
from jax.sharding import PartitionSpec as P

MESH = pl.DeviceIdType.MESH

epsilon = 1e-06


def layer_norm(values, norm_gain, norm_bias):
    row_mean = jnp.mean(values, axis=-1, keepdims=True)
    centred = values - row_mean
    variance = jnp.mean(centred * centred, axis=-1, keepdims=True)
    inv_std = lax.rsqrt(variance + epsilon)
    scaled = centred * inv_std
    return (scaled * norm_gain + norm_bias, scaled, inv_std)


def norm_back(upstream, scaled, inv_std):
    mean_up = jnp.mean(upstream, axis=-1, keepdims=True)
    mean_cross = jnp.mean(upstream * scaled, axis=-1, keepdims=True)
    return inv_std * (upstream - mean_up - scaled * mean_cross)


def gelu_parts(pre_act):
    normal_cdf = 0.5 * (1.0 + lax.erf(pre_act * 0.7071067811865476))
    density = jnp.exp(-0.5 * pre_act * pre_act) * 0.3989422804014327
    return (pre_act * normal_cdf, normal_cdf + pre_act * density)


def encode(enc_input, enc_params):
    (
        mlp_gain,
        mlp_bias,
        fc1_weight,
        fc1_bias,
        fc2_weight,
        fc2_bias,
        encoder_gain,
        encoder_bias,
        embed_weight,
        embed_bias,
    ) = enc_params
    rows_in = enc_input.astype(jnp.float32)
    mlp_in, mlp_scaled, mlp_inv = layer_norm(rows_in, mlp_gain, mlp_bias)
    mlp_in = mlp_in.astype(jnp.bfloat16)
    pre_act = jnp.dot(mlp_in, fc1_weight, preferred_element_type=jnp.float32) + fc1_bias
    activation, slope = gelu_parts(pre_act)
    hidden = activation.astype(jnp.bfloat16)
    encoded = rows_in + jnp.dot(hidden, fc2_weight, preferred_element_type=jnp.float32) + fc2_bias
    normed, enc_scaled, enc_inv = layer_norm(encoded, encoder_gain, encoder_bias)
    normed = normed.astype(jnp.bfloat16)
    projected = (
        jnp.dot(normed, embed_weight, preferred_element_type=jnp.float32) + embed_bias
    ).astype(jnp.bfloat16)
    saved = (mlp_in, mlp_scaled, mlp_inv, slope, hidden, enc_scaled, enc_inv)
    return (saved, projected)


def encode_back(saved, grad_compact, enc_params):
    (
        mlp_gain,
        mlp_bias,
        fc1_weight,
        fc1_bias,
        fc2_weight,
        fc2_bias,
        encoder_gain,
        encoder_bias,
        embed_weight,
        embed_bias,
    ) = enc_params
    mlp_in, mlp_scaled, mlp_inv, slope, hidden, enc_scaled, enc_inv = saved
    grad_normed = jnp.dot(grad_compact, embed_weight.T, preferred_element_type=jnp.float32)
    grad_encoded = norm_back(grad_normed * encoder_gain, enc_scaled, enc_inv).astype(jnp.bfloat16)
    grad_hidden = jnp.dot(grad_encoded, fc2_weight.T, preferred_element_type=jnp.float32)
    grad_pre = (grad_hidden * slope).astype(jnp.bfloat16)
    grad_mlp_in = jnp.dot(grad_pre, fc1_weight.T, preferred_element_type=jnp.float32)
    grad_feats = (
        grad_encoded.astype(jnp.float32) + norm_back(grad_mlp_in * mlp_gain, mlp_scaled, mlp_inv)
    ).astype(jnp.bfloat16)
    return (mlp_in, grad_pre, hidden, grad_encoded, grad_feats)


def decoder_pass(
    projected_rows,
    keep_rows,
    position_ids,
    upstream,
    position_table,
    mask_token,
    decoder_gain,
    decoder_bias,
):
    table_ids = jnp.arange(position_table.shape[0], dtype=jnp.int32)[None, :]
    pick = (position_ids[:, None] == table_ids).astype(jnp.bfloat16)
    placed = jnp.dot(pick, position_table, preferred_element_type=jnp.float32)
    dec_input = jnp.where(keep_rows, projected_rows, mask_token) + placed
    decoded, dec_scaled, dec_inv = layer_norm(dec_input, decoder_gain, decoder_bias)
    grad_input = norm_back(upstream.astype(jnp.float32) * decoder_gain, dec_scaled, dec_inv)
    grad_projected = jnp.where(keep_rows, grad_input, 0.0).astype(jnp.bfloat16)
    return (decoded.astype(jnp.bfloat16), grad_projected)


def reduce_kernel(
    chunks,
    z_count,
    lhs_a,
    rhs_a,
    lhs_b,
    rhs_b,
    weight,
    gain,
    scaled,
    inverse,
    scatter,
    out_a,
    out_b,
    feature_out,
    weight_held,
    upstream,
    grad_rows,
    turned_a,
    turned_b,
    gathered_a,
    gathered_b,
    acc_a,
    acc_b,
    send0_a,
    send0_b,
    land0_a,
    land0_b,
    land1_a,
    land1_b,
    land2_a,
    land2_b,
    land3_a,
    land3_b,
    pair_sems,
    z_sems,
    spread_sems,
    weight_sem,
):
    dp = lax.axis_index("dp")
    tile = lax.axis_index("tile")
    x = lax.rem(dp, 2)
    y = lax.div(dp, 2)
    core = lax.rem(tile, 2)
    my_z = lax.div(tile, 2)
    sibling = (dp, tile + 1 - 2 * core)
    across_x = (dp + 1 - 2 * x, tile)
    across_y = (dp + 2 - 4 * y, tile)
    diagonal = (3 - dp, tile)
    z_to = [lax.rem(my_z + k, z_count) for k in range(1, z_count)]
    peers = [sibling, across_x, across_y, diagonal]
    peers += [(dp, 2 * z + core) for z in z_to]

    fetch = pltpu.make_async_copy(weight, weight_held, weight_sem)
    fetch.start()
    barrier = pltpu.get_barrier_semaphore()
    for peer in peers:
        pl.semaphore_signal(barrier, inc=1, device_id=peer, device_id_type=MESH)
    pl.semaphore_wait(barrier, len(peers))

    tensors = (
        (turned_a, rhs_a, gathered_a, acc_a, send0_a, land0_a, send0_a, land1_a, send0_a, land2_a,
         send0_a, land3_a, x, y, across_x, across_y),
        (turned_b, rhs_b, gathered_b, acc_b, send0_b, land0_b, send0_b, land1_b, send0_b, land2_b,
         send0_b, land3_b, y, x, across_y, across_x),
    )
    copies = {}

    def send(key, src, dst, sems, at, peer):
        copy = pltpu.make_async_remote_copy(
            src_ref=src,
            dst_ref=dst,
            send_sem=sems.at[(0,) + at],
            recv_sem=sems.at[(1,) + at],
            device_id=peer,
            device_id_type=MESH,
        )
        copy.start()
        copies[key] = copy

    def products(t, j, which, store):
        lhs, rhs = tensors[t][0], tensors[t][1]
        rows = lhs.shape[0] // (2 * z_count)
        columns = rhs.shape[1] // chunks

        @pl.loop(0, z_count)
        def _(z):
            first = pl.multiple_of((2 * z + which) * rows, 16)
            part = jnp.dot(
                lhs[pl.ds(first, rows), :],
                rhs[:, j * columns : (j + 1) * columns],
                preferred_element_type=jnp.float32,
            )
            for e in range(4):
                if t == 0:
                    width = columns // 4
                    store(e // 2, e % 2, z, part[:, e * width : (e + 1) * width])
                else:
                    store(e // 2, e % 2, z, part[e * (rows // 4) : (e + 1) * (rows // 4)])

    def stage0(t, j):
        acc, send0, land0 = tensors[t][3:6]

        def store_send(f, g, z, value):
            send0[j, f, g, z] = value.astype(jnp.bfloat16)

        def store_own(f, g, z, value):
            acc[j, f, g, z] = value

        if j == 0:
            source = (lhs_a, lhs_b)[t]
            for at in range(0, source.shape[1], 256):
                tensors[t][0][at : at + 256, :] = source[:, at : at + 256].T
        products(t, j, 1 - core, store_send)
        send(("c", t, j), send0.at[j], land0.at[j], pair_sems, (0, t, j), sibling)
        products(t, j, core, store_own)

    def stage1(t, j):
        acc, _, land0, send1, land1 = tensors[t][3:8]
        f, partner = tensors[t][12], tensors[t][14]
        copies["c", t, j].wait()

        @pl.loop(0, z_count)
        def _(z):
            for g in range(2):
                send1[j, 0, g, z] = (
                    acc[j, 1 - f, g, z] + land0[j, 1 - f, g, z].astype(jnp.float32)
                ).astype(jnp.bfloat16)

        send(("f", t, j), send1.at[j, 0], land1.at[j], pair_sems, (1, t, j), partner)

        @pl.loop(0, z_count)
        def _(z):
            for g in range(2):
                acc[j, f, g, z] = acc[j, f, g, z] + land0[j, f, g, z].astype(jnp.float32)

    def stage2(t, j):
        acc = tensors[t][3]
        land1, send2, land2 = tensors[t][7:10]
        f, g, partner = tensors[t][12], tensors[t][13], tensors[t][15]
        copies["f", t, j].wait()

        @pl.loop(0, z_count)
        def _(z):
            send2[j, 1, 0, z] = (
                acc[j, f, 1 - g, z] + land1[j, 1 - g, z].astype(jnp.float32)
            ).astype(jnp.bfloat16)

        send(("g", t, j), send2.at[j, 1, 0], land2.at[j], pair_sems, (2, t, j), partner)

        @pl.loop(0, z_count)
        def _(z):
            acc[j, f, g, z] = acc[j, f, g, z] + land1[j, g, z].astype(jnp.float32)

    def stage3(t, j):
        acc = tensors[t][3]
        land2, send3, land3 = tensors[t][9:12]
        f, g = tensors[t][12], tensors[t][13]
        copies["g", t, j].wait()
        for k, z in enumerate(z_to):
            send3[j, 1, 1, k] = (acc[j, f, g, z] + land2[j, z].astype(jnp.float32)).astype(jnp.bfloat16)
            send(
                ("z", t, j, k), send3.at[j, 1, 1, k], land3.at[j, k], z_sems, (t, j, k),
                (dp, 2 * z + core),
            )
        acc[j, f, g, my_z] = acc[j, f, g, my_z] + land2[j, my_z].astype(jnp.float32)

    def stage4(t, j):
        out, acc = tensors[t][2:4]
        land3 = tensors[t][11]
        f, g = tensors[t][12], tensors[t][13]
        total = acc[j, f, g, my_z]
        for k in range(z_count - 1):
            copies["z", t, j, k].wait()
            total = total + land3[j, k].astype(jnp.float32)
        mine = 2 * f + g
        out[mine, j] = total.astype(jnp.bfloat16)
        for k, peer in enumerate((across_x, across_y, diagonal)):
            send(
                ("s", t, j, k), out.at[mine, j], out.at[mine, j], spread_sems, (t, j, k), peer
            )

    def stage5(t, j):
        gathered = tensors[t][2]
        for k in range(3):
            copies["s", t, j, k].wait()
        m, n = gathered.shape[2:]
        for e in range(4):
            if t == 0:
                out_a[:, (4 * j + e) * n : (4 * j + e + 1) * n] = gathered[e, j]
            else:
                out_b[e * m : (e + 1) * m, j * n : (j + 1) * n] = gathered[e, j]

    def feature_columns(q):
        if q == 0:
            fetch.wait()
        wide = weight_held.shape[0] // chunks
        at = slice(q * wide, (q + 1) * wide)
        part = lax.dot_general(
            rhs_a[...],
            weight_held[at, :],
            (((1,), (1,)), ((), ())),
            preferred_element_type=jnp.float32,
        )
        upstream[:, at] = part * gain[:, at]

    def feature_rows():
        block = upstream.shape[0] // 8

        @pl.loop(0, 8)
        def _(i):
            at = pl.ds(pl.multiple_of(i * block, block), block)
            back = norm_back(upstream[at, :], scaled[at, :], inverse[at, :])
            grad_rows[at, :] = (rhs_b[at, :].astype(jnp.float32) + back).astype(jnp.bfloat16)

        tall = feature_out.shape[0] // 4

        @pl.loop(0, 4)
        def _(i):
            at = pl.ds(pl.multiple_of(i * tall, tall), tall)
            feature_out[at, :] = jnp.dot(
                scatter[at, :], grad_rows[...], preferred_element_type=jnp.float32
            ).astype(jnp.bfloat16)

    stages = (stage0, stage1, stage2, stage3, stage4, stage5)
    for step in range(chunks + len(stages) - 1):
        for at in (1, 0, 2, 3, 4, 5):
            j = step - at
            if 0 <= j < chunks:
                for t in range(2):
                    stages[at](t, j)
        if 1 <= step <= chunks:
            feature_columns(step - 1)
        if step == chunks + 1:
            feature_rows()


def reduce_weights(
    mlp_in, grad_pre, hidden, grad_encoded, tiles, fc1_weight, mlp_gain, mlp_scaled, mlp_inv, scatter
):
    rows, width = mlp_in.shape
    inner = hidden.shape[1]
    z_count = tiles // 2
    rows_a, rows_b = width // tiles, inner // tiles // 4
    chunks = 5
    m_a, n_a = rows_a, inner // chunks // 4
    m_b, n_b = rows_b, width // chunks
    whole = pl.BlockSpec(memory_space=pltpu.VMEM)
    half, full = jnp.bfloat16, jnp.float32
    scratch = [
        pltpu.VMEM((width, inner), half),
        pltpu.VMEM((rows, width), full),
        pltpu.VMEM((rows, width), half),
        pltpu.VMEM((width, rows), half),
        pltpu.VMEM((inner, rows), half),
        pltpu.VMEM((4, chunks, m_a, n_a), half),
        pltpu.VMEM((4, chunks, m_b, n_b), half),
    ]
    for lead, kind in (
        ((2, 2, z_count), full),
        ((2, 2, z_count), half),
        ((2, 2, z_count), half),
        ((2, z_count), half),
        ((z_count,), half),
        ((z_count - 1,), half),
    ):
        for m, n in ((m_a, n_a), (m_b, n_b)):
            scratch.append(pltpu.VMEM((chunks,) + lead + (m, n), kind))
    scratch += [
        pltpu.SemaphoreType.DMA((2, 3, 2, chunks)),
        pltpu.SemaphoreType.DMA((2, 2, chunks, z_count - 1)),
        pltpu.SemaphoreType.DMA((2, 2, chunks, 3)),
        pltpu.SemaphoreType.DMA,
    ]
    out_a, out_b, features = pl.pallas_call(
        functools.partial(reduce_kernel, chunks, z_count),
        out_shape=(
            jax.ShapeDtypeStruct((rows_a, inner), half),
            jax.ShapeDtypeStruct((4 * rows_b, width), half),
            jax.ShapeDtypeStruct((scatter.shape[0], width), half),
        ),
        in_specs=[whole] * 4 + [pl.BlockSpec(memory_space=pl.ANY)] + [whole] * 4,
        out_specs=(whole, whole, whole),
        scratch_shapes=scratch,
        compiler_params=pltpu.CompilerParams(
            collective_id=0, has_side_effects=True, vmem_limit_bytes=56 * 2**20
        ),
    )(
        mlp_in,
        grad_pre,
        hidden,
        grad_encoded,
        fc1_weight,
        mlp_gain[None, :],
        mlp_scaled,
        mlp_inv,
        scatter,
    )
    return (out_a.astype(full), out_b.astype(full)), features


def reducible(mlp_in, hidden, scenes, tiles):
    width, inner = mlp_in.shape[1], hidden.shape[1]
    return (
        scenes == 4
        and tiles % 2 == 0
        and width % (tiles * 16) == 0
        and inner % (tiles * 4 * 16) == 0
        and inner % (5 * 4 * 128) == 0
        and width % (5 * 128) == 0
    )


def shards(
    features,
    visible,
    positions,
    cotangent,
    mlp_gain,
    mlp_bias,
    fc1_weight,
    fc1_bias,
    fc2_weight,
    fc2_bias,
    encoder_gain,
    encoder_bias,
    embed_weight,
    embed_bias,
    mask_token,
    position_table,
    decoder_gain,
    decoder_bias,
):
    patch_count = features.shape[2]
    model_width = features.shape[3]
    dec_width = embed_weight.shape[1]
    most_rows = patch_count // 2
    flags = visible.reshape(patch_count)
    row_data = features.reshape(patch_count, model_width)
    keep_rows = (flags > 0)[:, None]
    upstream = cotangent.reshape(patch_count, dec_width)
    ids = jnp.arange(patch_count, dtype=jnp.int32)
    row_rank = jnp.sum(jnp.where(ids[None, :] < ids[:, None], flags[None, :], 0), axis=1)
    slots = jnp.arange(most_rows, dtype=jnp.int32)
    target = jnp.where(flags > 0, row_rank, -1)
    gather = (slots[:, None] == target[None, :]).astype(jnp.bfloat16)
    scatter = (target[:, None] == slots[None, :]).astype(jnp.bfloat16)
    enc_params = (
        mlp_gain,
        mlp_bias,
        fc1_weight,
        fc1_bias,
        fc2_weight,
        fc2_bias,
        encoder_gain,
        encoder_bias,
        embed_weight,
        embed_bias,
    )
    decoder_args = (position_table, mask_token, decoder_gain, decoder_bias)
    enc_input = jnp.dot(gather, row_data, preferred_element_type=jnp.bfloat16)
    saved, projected = encode(enc_input, enc_params)
    projected_rows = jnp.dot(scatter, projected, preferred_element_type=jnp.float32)
    decoded, grad_projected = decoder_pass(
        projected_rows, keep_rows, positions.reshape(-1), upstream, *decoder_args
    )
    grad_compact = jnp.dot(gather, grad_projected, preferred_element_type=jnp.bfloat16)
    mlp_in, grad_pre, hidden, grad_encoded, grad_feats = encode_back(
        saved, grad_compact, enc_params
    )
    device_total = lax.axis_size("dp") * lax.axis_size("tile")
    tiles = lax.axis_size("tile")
    if reducible(mlp_in, hidden, lax.axis_size("dp"), tiles):
        totals, grad_rows = reduce_weights(
            mlp_in,
            grad_pre,
            hidden,
            grad_encoded,
            tiles,
            fc1_weight,
            mlp_gain,
            saved[1],
            saved[2],
            scatter,
        )
    else:
        grad_rows = jnp.dot(scatter, grad_feats, preferred_element_type=jnp.bfloat16)
        totals = []
        for left, right in ((mlp_in, grad_pre), (hidden, grad_encoded)):
            term = jnp.dot(left.T, right, preferred_element_type=jnp.float32)
            share = lax.psum_scatter(
                term.astype(jnp.bfloat16), "tile", scatter_dimension=0, tiled=True
            )
            totals.append(lax.psum(share, "dp").astype(jnp.float32))
    fc1_grad, fc2_grad = [total / device_total for total in totals]
    feature_grad = grad_rows.reshape(features.shape)
    decoded_out = decoded.reshape(cotangent.shape)
    return (feature_grad, decoded_out, fc1_grad, fc2_grad)


def solution(mesh):
    return jax.shard_map(
        shards,
        mesh=mesh,
        in_specs=(
            P("dp", "tile", None, None),
            P("dp", "tile", None),
            P("dp", "tile", None),
            P("dp", "tile", None, None),
            P(),
            P(),
            P(),
            P(),
            P(),
            P(),
            P(),
            P(),
            P(),
            P(),
            P(),
            P(),
            P(),
            P(),
        ),
        out_specs=(
            P("dp", "tile", None, None),
            P("dp", "tile", None, None),
            P("tile", None),
            P("tile", None),
        ),
        check_vma=False,
    )
```
